32 devices in a mesh: row: 4 (over y, x), col: 8 (over z, core).
Axes of the slice: x: 2, y: 2, z: 4, core: 2. Of those that a mesh axis runs over, the one named last changes fastest.
Arguments:
- dosages: bfloat16 [4, 1024, 16384], P(None, ('row', 'col')), may hold values from 0 to 2
- allele_counts: int32 [4, 1024], replicated, may hold values from 14745 to 18021
- slab_in: float32 [2048, 16384], P('row', 'col'), may hold values from -6 to 6
Outputs:
- slab_out: float32 [2048, 16384], P('row', 'col')
The draws below stay inside these ranges and needn't reach their ends.
All inputs are finite; a program needn't handle non-finite values.
Results may differ from the reference program's by a relative error of at most 0.002.
Values may be sent and summed in bfloat16 or wider, within the bound.
A program may use at most 192 MiB of HBM per device.

```python
import math
import jax
import jax.numpy as jnp
from jax import lax

SNPS = 1024
GROUPS = 4
ROWS = 2048
SAMPLES = 16384


def set_ends(values, own_key, low, high):
    extent = values.shape
    spot = [jax.random.randint(jax.random.fold_in(own_key, axis), (), 0, extent[axis]) for axis in range(len(extent))]
    values = values.at[tuple(spot)].set(low)
    longest = extent.index(max(extent))
    spot[longest] = (spot[longest] + 1) % extent[longest]
    return values.at[tuple(spot)].set(high)


def shard_levels(own_key, extent, cuts, least, top_value):
    def one(axis_at, shards_of):
        heights = jax.random.uniform(jax.random.fold_in(jax.random.fold_in(own_key, 6), axis_at), (shards_of,), jnp.float32, least / len(cuts), top_value / len(cuts))
        return jnp.repeat(jnp.exp(heights), extent[axis_at] // shards_of).reshape((-1,) + (1,) * (len(extent) - axis_at - 1))

    level = one(*cuts[0])
    for cut in cuts[1:]:
        level = level * one(*cut)
    return level


def bell_draw(rng, shape, scale, bound, cuts=(), kind=jnp.bfloat16):
    entries = jax.random.normal(rng, shape, jnp.float32) * scale
    if len(cuts) > 0:
        entries = shard_levels(rng, shape, cuts, -0.22, 0.18) * entries
    return jnp.clip(entries, min=-bound, max=bound).astype(kind)


def setup_inputs(seed: int = 0) -> dict:
    key_list = jax.random.split(jax.random.key(seed), 4)
    return {
        "dosages": jnp.clip(2.0 * jax.random.uniform(key_list[0], (GROUPS, SNPS, SAMPLES), jnp.float32) ** shard_levels(key_list[0], (GROUPS, SNPS, SAMPLES), ((1, 32),), -0.2, 0.2), 0.0, 2.0).astype(jnp.bfloat16),
        "allele_counts": set_ends(jax.random.randint(key_list[1], (GROUPS, SNPS), 9 * SAMPLES // 10, 11 * SAMPLES // 10), jax.random.fold_in(key_list[1], 1), 9 * SAMPLES // 10, (11 * SAMPLES // 10) - 1).astype(jnp.int32),
        "slab_in": bell_draw(key_list[2], (ROWS, SAMPLES), 1.0, 6.0, ((0, 4), (1, 8)), jnp.float32),
    }


def standardize(dosage_block, count_row):
    frequency = count_row.astype(jnp.float32) / (2.0 * SAMPLES)
    centre = 2.0 * frequency
    spread = jnp.sqrt(2.0 * frequency * (1.0 - frequency))
    return ((dosage_block.astype(jnp.float32) - centre[:, None]) / spread[:, None]).astype(jnp.bfloat16)

def reference(dosages, allele_counts, slab_in):
    factor = 1.0 / math.sqrt(GROUPS * SNPS)
    total = slab_in
    for group_index in range(GROUPS):
        scaled = standardize(dosages[group_index], allele_counts[group_index]).astype(jnp.float32)
        product = jnp.dot(scaled[:, :ROWS].T, scaled, precision=lax.Precision.HIGHEST)
        total = total + factor * product
    return total
```

```python
import functools
import math

import jax
import jax.numpy as jnp
from jax import lax
from jax.experimental import pallas as pl
from jax.experimental.pallas import tpu as pltpu
from jax.sharding import PartitionSpec as P

LANES = 128
FILL = (1, 2, 3, 4)
LEAD = 4
LAG = 2
LATE_STEP = 2
VMEM_BYTES = 48 * 1024 * 1024
MESH = pl.DeviceIdType.MESH


def moments(count, total_samples):
    frequency = count.astype(jnp.float32) / (2.0 * total_samples)
    return 2.0 * frequency, jnp.sqrt(2.0 * frequency * (1.0 - frequency))


def standardize(dosage_block, count_row, total_samples):
    centre, spread = moments(count_row, total_samples)
    return ((dosage_block.astype(jnp.float32) - centre[..., None]) / spread[..., None]).astype(
        jnp.bfloat16
    )


def kernel(
    factor, cols_n, chunks,
    source, ordered, slab, out,
    centre, scale, rows_raw, rows_t, cols, keep_a, keep_b, final,
    send_a, send_b, got_a, got_b, send2_a, send2_b, got2_a, got2_b,
    rows_send, rows_recv, rows_own_sem, cols_send, cols_recv, cols_own,
    s1_send, s1_recv, s2_send, s2_recv, out_sem, slab_sem,
):
    r = lax.axis_index("row")
    c = lax.axis_index("col")
    depth = source.shape[0]
    chips = cols_n // 2
    core = lax.rem(c, 2)
    z = c // 2
    partner = c + 1 - 2 * core
    width = out.shape[1]
    wide = width // chunks
    block_rows = out.shape[0]
    r1 = r + 1 - 2 * lax.rem(r, 2)
    r2 = lax.rem(r + 2, 4)
    r3 = lax.rem(r1 + 2, 4)
    blocks = (r3, r1, r2, r)
    early = (0, 1, 2)
    late = 3

    def at_col(col):
        return {"row": r, "col": col}

    def at_row(row):
        return {"row": row, "col": c}

    barrier = pltpu.get_barrier_semaphore()
    for step in range(1, cols_n):
        pl.semaphore_signal(
            barrier, 1, device_id=at_col(lax.rem(c + step, cols_n)), device_id_type=MESH
        )
    for row in (r1, r2):
        pl.semaphore_signal(barrier, 1, device_id=at_row(row), device_id_type=MESH)
    pl.semaphore_wait(barrier, cols_n + 1)

    def slot_rows(slot):
        return pl.ds(pl.multiple_of(slot * depth, depth), depth)

    def own_block(j):
        return source.at[:, pl.ds(pl.multiple_of(blocks[j] * block_rows, block_rows), block_rows)]

    def rows_copy(j, slot, target, way, first):
        place = rows_raw.at[j, slot_rows(slot)]
        return pltpu.make_async_remote_copy(
            src_ref=own_block(j) if first else place,
            dst_ref=place,
            send_sem=rows_send.at[way, j, slot],
            recv_sem=rows_recv.at[j, slot],
            device_id=at_col(target),
            device_id_type=MESH,
        )

    def rows_arrived(j, slot):
        rows_copy(j, slot, partner, 2, False).wait_recv()

    up, down = lax.rem(c + 2, cols_n), lax.rem(c + cols_n - 2, cols_n)

    def send_rows(j, slot, first, go_up, go_down):
        @pl.when(go_up)
        def _():
            rows_copy(j, slot, up, 0, first).start()

        @pl.when(go_down)
        def _():
            rows_copy(j, slot, down, 1, first).start()

        rows_copy(j, slot, partner, 2, first).start()

    def own_rows(j):
        return pltpu.make_async_copy(
            own_block(j), rows_raw.at[j, slot_rows(c)], rows_own_sem.at[j]
        )

    def first_rows(j):
        own_rows(j).start()
        send_rows(j, c, True, z + 1 < chips, z > 0)

    def forward_rows(j, distance):
        @pl.when(z >= distance)
        def _():
            rows_arrived(j, c - 2 * distance)
            send_rows(j, c - 2 * distance, False, z + 1 < chips, z < 0)

        @pl.when(z + distance < chips)
        def _():
            rows_arrived(j, c + 2 * distance)
            send_rows(j, c + 2 * distance, False, z < 0, z > 0)

    def columns_copy(q, step):
        target = lax.rem(c + step, cols_n)
        return pltpu.make_async_remote_copy(
            src_ref=source.at[:, pl.ds(pl.multiple_of(target * width + q * wide, wide), wide)],
            dst_ref=cols.at[q, slot_rows(c)],
            send_sem=cols_send.at[q],
            recv_sem=cols_recv.at[q],
            device_id=at_col(target),
            device_id_type=MESH,
        )

    def own_columns(q):
        return pltpu.make_async_copy(
            source.at[:, pl.ds(pl.multiple_of(c * width + q * wide, wide), wide)],
            cols.at[q, slot_rows(c)],
            cols_own.at[q],
        )

    def send_columns(q):
        for step in range(1, cols_n):
            columns_copy(q, step).start()
        own_columns(q).start()

    def turn_rows(j, slot):
        place = slot_rows(slot)
        for start in range(0, block_rows, LANES):
            raw = rows_raw[j, place, pl.ds(start, LANES)].astype(jnp.float32)
            value = (raw - centre[place, :]) * scale[place, :]
            rows_t[j, pl.ds(start, LANES), place] = value.T.astype(jnp.bfloat16)

    def turn_own(j):
        own_rows(j).wait()
        turn_rows(j, c)

    def turn_partner(j):
        rows_arrived(j, partner)
        turn_rows(j, partner)

    def turn_at(j, distance):
        @pl.when(z >= distance)
        def _():
            turn_rows(j, c - 2 * distance)
            rows_arrived(j, partner - 2 * distance)
            turn_rows(j, partner - 2 * distance)

        @pl.when(z + distance < chips)
        def _():
            turn_rows(j, c + 2 * distance)
            rows_arrived(j, partner + 2 * distance)
            turn_rows(j, partner + 2 * distance)

    for j in early:
        first_rows(j)
    for q in range(FILL[0]):
        send_columns(q)
    for slot in range(cols_n):
        middle, spread = moments(ordered[pl.ds(slot, 1), :], source.shape[1])
        place = pl.ds(slot * depth, depth)
        centre[place, :] = jnp.broadcast_to(middle, (LANES, depth)).T
        scale[place, :] = jnp.broadcast_to(1.0 / spread, (LANES, depth)).T
    for j in early:
        turn_own(j)
    for distance in range(1, chips):
        for j in early:
            forward_rows(j, distance)
        for q in range(FILL[distance - 1], FILL[distance]):
            send_columns(q)
        for j in early:
            if distance == 1:
                turn_partner(j)
            else:
                turn_at(j, distance - 1)
    for j in early:
        turn_at(j, chips - 1)

    begun = FILL[chips - 1]

    def slab_copy(q):
        place = pl.ds(pl.multiple_of(q * wide, wide), wide)
        return pltpu.make_async_copy(slab.at[:, place], final.at[q], slab_sem.at[q])

    for q in range(chunks):
        slab_copy(q).start()

    def exchange(src, dst, sends, recvs, q, side, row):
        return pltpu.make_async_remote_copy(
            src_ref=src.at[q],
            dst_ref=dst.at[q],
            send_sem=sends.at[side, q],
            recv_sem=recvs.at[side, q],
            device_id=at_row(row),
            device_id_type=MESH,
        )

    def first_a(q):
        return exchange(send_a, got_a, s1_send, s1_recv, q, 0, r1)

    def first_b(q):
        return exchange(send_b, got_b, s1_send, s1_recv, q, 1, r2)

    def second_a(q):
        return exchange(send2_a, got2_a, s2_send, s2_recv, q, 0, r2)

    def second_b(q):
        return exchange(send2_b, got2_b, s2_send, s2_recv, q, 1, r1)

    half = out.shape[0] // 2

    def columns_received(q):
        place = cols.at[q, pl.ds(0, (cols_n - 1) * depth)]
        pltpu.make_async_copy(place, place, cols_recv.at[q]).wait()
        own_columns(q).wait()

    def product(j, q):
        return jnp.dot(rows_t[j], cols[q], preferred_element_type=jnp.float32)

    def produce(q):
        columns_received(q)
        for slot in range(cols_n):
            place = pl.ds(slot * depth, depth)
            for start in range(0, wide, LANES):
                raw = cols[q, place, pl.ds(start, LANES)].astype(jnp.float32)
                value = (raw - centre[place, :]) * scale[place, :]
                cols[q, place, pl.ds(start, LANES)] = value.astype(jnp.bfloat16)
        far = product(0, q)
        send_a[q, 1] = far[:half].astype(jnp.bfloat16)
        send_b[q, 1] = far[half:].astype(jnp.bfloat16)
        near = product(1, q)
        send_a[q, 0] = near[:half].astype(jnp.bfloat16)
        keep_b[lax.rem(q, LAG + 1)] = near[half:]
        first_a(q).start()
        near = product(2, q)
        send_b[q, 0] = near[half:].astype(jnp.bfloat16)
        keep_a[lax.rem(q, LAG + 1)] = near[:half]
        first_b(q).start()

    def combine(q):
        first_a(q).wait_recv()
        send2_a[q] = (keep_a[lax.rem(q, LAG + 1)] + got_a[q, 1].astype(jnp.float32)).astype(jnp.bfloat16)
        second_a(q).start()
        first_b(q).wait_recv()
        send2_b[q] = (keep_b[lax.rem(q, LAG + 1)] + got_b[q, 1].astype(jnp.float32)).astype(jnp.bfloat16)
        second_b(q).start()

    def out_copy(q):
        place = pl.ds(pl.multiple_of(q * wide, wide), wide)
        return pltpu.make_async_copy(final.at[q], out.at[:, place], out_sem.at[q])

    def finish(q):
        own = product(late, q)
        slab_copy(q).wait()
        second_a(q).wait_recv()
        final[q, :half] += factor * (
            own[:half]
            + got_a[q, 0].astype(jnp.float32)
            + got2_a[q].astype(jnp.float32)
        )
        second_b(q).wait_recv()
        final[q, half:] += factor * (
            own[half:]
            + got_b[q, 0].astype(jnp.float32)
            + got2_b[q].astype(jnp.float32)
        )
        out_copy(q).start()

    hops = tuple(min(LATE_STEP * distance, chunks // 2) for distance in range(chips + 1))
    settle = hops[chips]

    def finished(q):
        return jnp.maximum(jnp.minimum(2 * (q - settle + 1), q - 2 * LAG + 1), 0)

    def step(q, carry):
        @pl.when((q + LEAD >= begun) & (q + LEAD < chunks))
        def _():
            send_columns(q + LEAD)

        for distance in range(1, chips):

            @pl.when(q == hops[distance])
            def _():
                forward_rows(late, distance)

        @pl.when(q < chunks)
        def _():
            produce(q)

        @pl.when((q >= LAG) & (q < chunks + LAG))
        def _():
            combine(q - LAG)

        @pl.when(q == settle)
        def _():
            turn_own(late)
            turn_partner(late)
            for distance in range(1, chips):
                turn_at(late, distance)

        begin, end = finished(q - 1), finished(q)
        for extra in range(2):

            @pl.when(begin + extra < end)
            def _():
                finish(begin + extra)

        return carry

    first_rows(late)
    lax.fori_loop(0, chunks + 2 * LAG, step, 0)

    for j in range(4):
        rows_copy(j, c, partner, 2, True).wait_send()

        @pl.when(z + 1 < chips)
        def _():
            rows_copy(j, c, up, 0, True).wait_send()

        @pl.when(z > 0)
        def _():
            rows_copy(j, c, down, 1, True).wait_send()

        for distance in range(1, chips):
            below, above = c - 2 * distance, c + 2 * distance

            @pl.when(z >= distance)
            def _():
                rows_copy(j, below, partner, 2, False).wait_send()

            @pl.when((z >= distance) & (z + 1 < chips))
            def _():
                rows_copy(j, below, up, 0, False).wait_send()

            @pl.when(z + distance < chips)
            def _():
                rows_copy(j, above, partner, 2, False).wait_send()

            @pl.when((z + distance < chips) & (z > 0))
            def _():
                rows_copy(j, above, down, 1, False).wait_send()

    def drain(q, carry):
        sent = cols.at[q, pl.ds(0, (cols_n - 1) * depth)]
        pltpu.make_async_copy(sent, sent, cols_send.at[q]).wait()
        first_a(q).wait_send()
        first_b(q).wait_send()
        second_a(q).wait_send()
        second_b(q).wait_send()
        out_copy(q).wait()
        return carry

    lax.fori_loop(0, chunks, drain, 0)


def scratch_of(depth, cols_n, chunks, wide, slab_rows, block_rows):
    held = depth * cols_n
    half = block_rows // 2
    bf16, f32 = jnp.bfloat16, jnp.float32
    return [
        ((held, LANES), f32),
        ((held, LANES), f32),
        ((slab_rows // block_rows, held, block_rows), bf16),
        ((slab_rows // block_rows, block_rows, held), bf16),
        ((chunks, held, wide), bf16),
        ((LAG + 1, half, wide), f32),
        ((LAG + 1, half, wide), f32),
        ((chunks, block_rows, wide), f32),
        ((chunks, 2, half, wide), bf16),
        ((chunks, 2, half, wide), bf16),
        ((chunks, 2, half, wide), bf16),
        ((chunks, 2, half, wide), bf16),
        ((chunks, half, wide), bf16),
        ((chunks, half, wide), bf16),
        ((chunks, half, wide), bf16),
        ((chunks, half, wide), bf16),
    ]


def chunked(groups, own, counts, total_samples, dosages, slab_in, factor, rows_n, cols_n):
    held = own * cols_n
    slab_rows = slab_in.shape[0] * rows_n
    rows = lax.all_gather(dosages[:, :, :slab_rows], "col", axis=1, tiled=True)
    rows = standardize(rows, counts, total_samples)
    width = slab_in.shape[1]
    chunk = min(1024, width)
    sources = dosages.reshape(groups, own, cols_n, width)
    updates = []
    for start in range(0, width, chunk):
        columns = lax.all_to_all(
            sources[..., start : start + chunk], "col", split_axis=2, concat_axis=1, tiled=True
        ).reshape(groups, held, chunk)
        partial = lax.dot_general(
            rows,
            standardize(columns, counts, total_samples),
            (((0, 1), (0, 1)), ((), ())),
            preferred_element_type=jnp.float32,
        )
        updates.append(lax.psum_scatter(factor * partial, "row", scatter_dimension=0, tiled=True))
    return slab_in + jnp.concatenate(updates, axis=1)


def local(dosages, allele_counts, slab_in):
    groups, own, total_samples = dosages.shape
    snp_count = allele_counts.shape[1]
    rows_n = lax.axis_size("row")
    cols_n = lax.axis_size("col")
    factor = 1.0 / math.sqrt(groups * snp_count)
    held = own * cols_n
    depth = groups * own
    block_rows, width = slab_in.shape
    slab_rows = block_rows * rows_n
    counts = lax.dynamic_slice_in_dim(allele_counts, lax.axis_index("row") * held, held, axis=1)
    wide = LANES
    chunks = width // wide
    scratch = scratch_of(depth, cols_n, max(chunks, 1), wide, slab_rows, block_rows)
    size = sum(math.prod(shape) * jnp.dtype(kind).itemsize for shape, kind in scratch)
    fits = (
        rows_n == 4
        and cols_n % 2 == 0
        and depth % LANES == 0
        and own % 16 == 0
        and width % wide == 0
        and block_rows % (2 * LANES) == 0
        and chunks >= 4
        and size + 16 * 1024 * 1024 <= VMEM_BYTES
    )
    if not fits:
        return chunked(
            groups, own, counts, total_samples, dosages, slab_in, factor, rows_n, cols_n
        )
    ordered = counts.reshape(groups, cols_n, own).transpose(1, 0, 2).reshape(cols_n, depth)
    dma = pltpu.SemaphoreType.DMA
    return pl.pallas_call(
        functools.partial(kernel, factor, cols_n, chunks),
        out_shape=jax.ShapeDtypeStruct((block_rows, width), jnp.float32),
        in_specs=[
            pl.BlockSpec(memory_space=pl.ANY),
            pl.BlockSpec(memory_space=pltpu.VMEM),
            pl.BlockSpec(memory_space=pl.ANY),
        ],
        out_specs=pl.BlockSpec(memory_space=pl.ANY),
        scratch_shapes=[pltpu.VMEM(shape, kind) for shape, kind in scratch]
        + [
            dma((3, 4, cols_n)), dma((4, cols_n)), dma((4,)), dma((chunks,)), dma((chunks,)), dma((chunks,)),
            dma((2, chunks)), dma((2, chunks)), dma((2, chunks)), dma((2, chunks)), dma((chunks,)),
            dma((chunks,)),
        ],
        compiler_params=pltpu.CompilerParams(
            collective_id=0, has_side_effects=True, vmem_limit_bytes=VMEM_BYTES
        ),
    )(dosages.reshape(depth, total_samples), ordered, slab_in)


def solution(mesh):
    placed = (P(None, ("row", "col"), None), P(), P("row", "col"))
    return jax.shard_map(
        local, mesh=mesh, in_specs=placed, out_specs=P("row", "col"), check_vma=False
    )
```

```python
import functools
import math

import jax
import jax.numpy as jnp
from jax import lax
from jax.experimental import pallas as pl
from jax.experimental.pallas import tpu as pltpu
from jax.sharding import PartitionSpec as P

LANES = 128
FILL = (0, 1, 2, 3)
LEAD = 3
LAG = 1
LATE_STEP = 2
VMEM_BYTES = 48 * 1024 * 1024
MESH = pl.DeviceIdType.MESH


def moments(count, total_samples):
    frequency = count.astype(jnp.float32) / (2.0 * total_samples)
    return 2.0 * frequency, jnp.sqrt(2.0 * frequency * (1.0 - frequency))


def standardize(dosage_block, count_row, total_samples):
    centre, spread = moments(count_row, total_samples)
    return ((dosage_block.astype(jnp.float32) - centre[..., None]) / spread[..., None]).astype(
        jnp.bfloat16
    )


def kernel(
    factor, cols_n, chunks, own,
    source, counts, slab, out,
    tally, centre, scale, rows_raw, rows_t, cols, keep_a, keep_b, final,
    send_a, send_b, got_a, got_b, send2_a, send2_b, got2_a, got2_b,
    rows_send, rows_recv, rows_own_sem, cols_send, cols_recv, cols_own,
    s1_send, s1_recv, s2_send, s2_recv, out_sem, slab_sem, tally_sem, word,
):
    r = lax.axis_index("row")
    c = lax.axis_index("col")
    depth = source.shape[0]
    chips = cols_n // 2
    core = lax.rem(c, 2)
    z = c // 2
    partner = c + 1 - 2 * core
    width = out.shape[1]
    wide = width // chunks
    block_rows = out.shape[0]
    r1 = r + 1 - 2 * lax.rem(r, 2)
    r2 = lax.rem(r + 2, 4)
    r3 = lax.rem(r1 + 2, 4)
    blocks = (r3, r1, r2, r)
    early = (0, 1, 2)
    late = 3

    def at_col(col):
        return {"row": r, "col": col}

    def at_row(row):
        return {"row": row, "col": c}

    tally_copy = pltpu.make_async_copy(counts, tally, tally_sem)
    tally_copy.start()
    barrier = pltpu.get_barrier_semaphore()
    up, down = lax.rem(c + 2, cols_n), lax.rem(c + cols_n - 2, cols_n)
    has_up, has_down = z + 1 < chips, z > 0

    def greet(semaphore, target):
        pl.semaphore_signal(semaphore, 1, device_id=target, device_id_type=MESH)

    pl.when(has_up)(lambda: greet(barrier, at_col(up)))
    pl.when(has_down)(lambda: greet(barrier, at_col(down)))
    for target in (at_col(partner), at_row(r1), at_row(r2)):
        greet(barrier, target)
    pl.semaphore_wait(barrier, 3 + has_up.astype(jnp.int32) + has_down.astype(jnp.int32))

    def ready():
        for wave in range(chips - 1):
            pl.when(has_up)(lambda: greet(word.at[0, wave], at_col(up)))
            pl.when(has_down)(lambda: greet(word.at[1, wave], at_col(down)))
            pl.when(has_down)(lambda: pl.semaphore_wait(word.at[0, wave], 1))
            pl.when(has_up)(lambda: pl.semaphore_wait(word.at[1, wave], 1))

    def slot_rows(slot):
        return pl.ds(pl.multiple_of(slot * depth, depth), depth)

    def own_block(j):
        return source.at[:, pl.ds(pl.multiple_of(blocks[j] * block_rows, block_rows), block_rows)]

    def rows_copy(j, slot, target, way, first):
        place = rows_raw.at[j, slot_rows(slot)]
        return pltpu.make_async_remote_copy(
            src_ref=own_block(j) if first else place,
            dst_ref=place,
            send_sem=rows_send.at[way, j, slot],
            recv_sem=rows_recv.at[j, slot],
            device_id=at_col(target),
            device_id_type=MESH,
        )

    def rows_arrived(j, slot):
        rows_copy(j, slot, partner, 2, False).wait_recv()

    def send_rows(j, slot, first, go_up, go_down):
        @pl.when(go_up)
        def _():
            rows_copy(j, slot, up, 0, first).start()

        @pl.when(go_down)
        def _():
            rows_copy(j, slot, down, 1, first).start()

        rows_copy(j, slot, partner, 2, first).start()

    def own_rows(j):
        return pltpu.make_async_copy(
            own_block(j), rows_raw.at[j, slot_rows(c)], rows_own_sem.at[j]
        )

    def first_rows(j):
        own_rows(j).start()
        send_rows(j, c, True, z + 1 < chips, z > 0)

    def forward_rows(j, distance):
        @pl.when(z >= distance)
        def _():
            rows_arrived(j, c - 2 * distance)
            send_rows(j, c - 2 * distance, False, z + 1 < chips, z < 0)

        @pl.when(z + distance < chips)
        def _():
            rows_arrived(j, c + 2 * distance)
            send_rows(j, c + 2 * distance, False, z < 0, z > 0)

    def columns_copy(q, step):
        target = lax.rem(c + step, cols_n)
        return pltpu.make_async_remote_copy(
            src_ref=source.at[:, pl.ds(pl.multiple_of(target * width + q * wide, wide), wide)],
            dst_ref=cols.at[q, slot_rows(c)],
            send_sem=cols_send.at[q],
            recv_sem=cols_recv.at[q],
            device_id=at_col(target),
            device_id_type=MESH,
        )

    def own_columns(q):
        return pltpu.make_async_copy(
            source.at[:, pl.ds(pl.multiple_of(c * width + q * wide, wide), wide)],
            cols.at[q, slot_rows(c)],
            cols_own.at[q],
        )

    def send_columns(q):
        for step in range(1, cols_n):
            columns_copy(q, step).start()
        own_columns(q).start()

    def turn_rows(j, slot):
        place = slot_rows(slot)
        for start in range(0, block_rows, LANES):
            raw = rows_raw[j, place, pl.ds(start, LANES)].astype(jnp.float32)
            value = (raw - centre[place, :]) * scale[place, :]
            rows_t[j, pl.ds(start, LANES), place] = value.T.astype(jnp.bfloat16)

    def turn_own(j):
        own_rows(j).wait()
        turn_rows(j, c)

    def turn_partner(j):
        rows_arrived(j, partner)
        turn_rows(j, partner)

    def turn_at(j, distance):
        @pl.when(z >= distance)
        def _():
            turn_rows(j, c - 2 * distance)
            rows_arrived(j, partner - 2 * distance)
            turn_rows(j, partner - 2 * distance)

        @pl.when(z + distance < chips)
        def _():
            turn_rows(j, c + 2 * distance)
            rows_arrived(j, partner + 2 * distance)
            turn_rows(j, partner + 2 * distance)

    for j in early:
        first_rows(j)
    tally_copy.wait()
    line = own * cols_n
    for group in range(depth // own):
        count = tally[pl.ds(group, 1), pl.ds(pl.multiple_of(r * line, LANES), line)]
        middle, spread = moments(count, source.shape[1])
        middle = jnp.broadcast_to(middle, (LANES, line)).T
        spread = jnp.broadcast_to(1.0 / spread, (LANES, line)).T
        for slot in range(cols_n):
            place = pl.ds(slot * depth + group * own, own)
            centre[place, :] = middle[slot * own : (slot + 1) * own]
            scale[place, :] = spread[slot * own : (slot + 1) * own]
    ready()
    for q in range(FILL[0]):
        send_columns(q)
    for j in early:
        turn_own(j)
    for distance in range(1, chips):
        for j in early:
            forward_rows(j, distance)
        for q in range(FILL[distance - 1], FILL[distance]):
            send_columns(q)
        for j in early:
            if distance == 1:
                turn_partner(j)
            else:
                turn_at(j, distance - 1)
    for j in early:
        turn_at(j, chips - 1)

    begun = FILL[chips - 1]

    def slab_copy(q):
        place = pl.ds(pl.multiple_of(q * wide, wide), wide)
        return pltpu.make_async_copy(slab.at[:, place], final.at[q], slab_sem.at[q])

    for q in range(chunks):
        slab_copy(q).start()

    def exchange(src, dst, at, sends, recvs, q, side, row):
        return pltpu.make_async_remote_copy(
            src_ref=src.at[at],
            dst_ref=dst.at[at],
            send_sem=sends.at[side, q],
            recv_sem=recvs.at[side, q],
            device_id=at_row(row),
            device_id_type=MESH,
        )

    def far_a(q):
        return exchange(send_a, got_a, (q, 1), s1_send, s1_recv, q, 0, r1)

    def far_b(q):
        return exchange(send_b, got_b, (q, 1), s1_send, s1_recv, q, 1, r2)

    def near_a(q):
        return exchange(send_a, got_a, (q, 0), s1_send, s1_recv, q, 2, r1)

    def near_b(q):
        return exchange(send_b, got_b, (q, 0), s1_send, s1_recv, q, 3, r2)

    def second_a(q):
        return exchange(send2_a, got2_a, (q,), s2_send, s2_recv, q, 0, r2)

    def second_b(q):
        return exchange(send2_b, got2_b, (q,), s2_send, s2_recv, q, 1, r1)

    half = out.shape[0] // 2

    def columns_received(q):
        place = cols.at[q, pl.ds(0, (cols_n - 1) * depth)]
        pltpu.make_async_copy(place, place, cols_recv.at[q]).wait()
        own_columns(q).wait()

    def product(j, q):
        return jnp.dot(rows_t[j], cols[q], preferred_element_type=jnp.float32)

    def produce(q):
        columns_received(q)
        for slot in range(cols_n):
            place = pl.ds(slot * depth, depth)
            for start in range(0, wide, LANES):
                raw = cols[q, place, pl.ds(start, LANES)].astype(jnp.float32)
                value = (raw - centre[place, :]) * scale[place, :]
                cols[q, place, pl.ds(start, LANES)] = value.astype(jnp.bfloat16)
        far = product(0, q)
        send_a[q, 1] = far[:half].astype(jnp.bfloat16)
        far_a(q).start()
        send_b[q, 1] = far[half:].astype(jnp.bfloat16)
        far_b(q).start()
        near = product(1, q)
        send_a[q, 0] = near[:half].astype(jnp.bfloat16)
        near_a(q).start()
        keep_b[lax.rem(q, LAG + 1)] = near[half:]
        near = product(2, q)
        send_b[q, 0] = near[half:].astype(jnp.bfloat16)
        near_b(q).start()
        keep_a[lax.rem(q, LAG + 1)] = near[:half]

    def combine(q):
        far_a(q).wait_recv()
        send2_a[q] = (keep_a[lax.rem(q, LAG + 1)] + got_a[q, 1].astype(jnp.float32)).astype(jnp.bfloat16)
        second_a(q).start()
        far_b(q).wait_recv()
        send2_b[q] = (keep_b[lax.rem(q, LAG + 1)] + got_b[q, 1].astype(jnp.float32)).astype(jnp.bfloat16)
        second_b(q).start()

    def out_copy(q):
        place = pl.ds(pl.multiple_of(q * wide, wide), wide)
        return pltpu.make_async_copy(final.at[q], out.at[:, place], out_sem.at[q])

    def finish(q):
        own = product(late, q)
        slab_copy(q).wait()
        near_a(q).wait_recv()
        second_a(q).wait_recv()
        final[q, :half] += factor * (
            own[:half]
            + got_a[q, 0].astype(jnp.float32)
            + got2_a[q].astype(jnp.float32)
        )
        near_b(q).wait_recv()
        second_b(q).wait_recv()
        final[q, half:] += factor * (
            own[half:]
            + got_b[q, 0].astype(jnp.float32)
            + got2_b[q].astype(jnp.float32)
        )
        out_copy(q).start()

    hops = tuple(min(LATE_STEP * distance, chunks // 2) for distance in range(chips + 1))
    settle = hops[chips]

    def finished(q):
        return jnp.maximum(jnp.minimum(2 * (q - settle + 1), q - 2 * LAG + 1), 0)

    def step(q, carry):
        @pl.when((q + LEAD >= begun) & (q + LEAD < chunks))
        def _():
            send_columns(q + LEAD)

        for distance in range(1, chips):

            @pl.when(q == hops[distance])
            def _():
                forward_rows(late, distance)

        @pl.when(q < chunks)
        def _():
            produce(q)

        @pl.when((q >= LAG) & (q < chunks + LAG))
        def _():
            combine(q - LAG)

        @pl.when(q == settle)
        def _():
            turn_own(late)
            turn_partner(late)
            for distance in range(1, chips):
                turn_at(late, distance)

        begin, end = finished(q - 1), finished(q)
        for extra in range(2):

            @pl.when(begin + extra < end)
            def _():
                finish(begin + extra)

        return carry

    first_rows(late)
    lax.fori_loop(0, chunks + 2 * LAG, step, 0)

    for j in range(4):
        rows_copy(j, c, partner, 2, True).wait_send()

        @pl.when(z + 1 < chips)
        def _():
            rows_copy(j, c, up, 0, True).wait_send()

        @pl.when(z > 0)
        def _():
            rows_copy(j, c, down, 1, True).wait_send()

        for distance in range(1, chips):
            below, above = c - 2 * distance, c + 2 * distance

            @pl.when(z >= distance)
            def _():
                rows_copy(j, below, partner, 2, False).wait_send()

            @pl.when((z >= distance) & (z + 1 < chips))
            def _():
                rows_copy(j, below, up, 0, False).wait_send()

            @pl.when(z + distance < chips)
            def _():
                rows_copy(j, above, partner, 2, False).wait_send()

            @pl.when((z + distance < chips) & (z > 0))
            def _():
                rows_copy(j, above, down, 1, False).wait_send()

    def drain(q, carry):
        sent = cols.at[q, pl.ds(0, (cols_n - 1) * depth)]
        pltpu.make_async_copy(sent, sent, cols_send.at[q]).wait()
        far_a(q).wait_send()
        far_b(q).wait_send()
        near_a(q).wait_send()
        near_b(q).wait_send()
        second_a(q).wait_send()
        second_b(q).wait_send()
        out_copy(q).wait()
        return carry

    lax.fori_loop(0, chunks, drain, 0)


def scratch_of(depth, cols_n, chunks, wide, slab_rows, block_rows):
    held = depth * cols_n
    half = block_rows // 2
    bf16, f32 = jnp.bfloat16, jnp.float32
    return [
        ((held, LANES), f32),
        ((held, LANES), f32),
        ((slab_rows // block_rows, held, block_rows), bf16),
        ((slab_rows // block_rows, block_rows, held), bf16),
        ((chunks, held, wide), bf16),
        ((LAG + 1, half, wide), f32),
        ((LAG + 1, half, wide), f32),
        ((chunks, block_rows, wide), f32),
        ((chunks, 2, half, wide), bf16),
        ((chunks, 2, half, wide), bf16),
        ((chunks, 2, half, wide), bf16),
        ((chunks, 2, half, wide), bf16),
        ((chunks, half, wide), bf16),
        ((chunks, half, wide), bf16),
        ((chunks, half, wide), bf16),
        ((chunks, half, wide), bf16),
    ]


def chunked(groups, own, counts, total_samples, dosages, slab_in, factor, rows_n, cols_n):
    held = own * cols_n
    slab_rows = slab_in.shape[0] * rows_n
    rows = lax.all_gather(dosages[:, :, :slab_rows], "col", axis=1, tiled=True)
    rows = standardize(rows, counts, total_samples)
    width = slab_in.shape[1]
    chunk = min(1024, width)
    sources = dosages.reshape(groups, own, cols_n, width)
    updates = []
    for start in range(0, width, chunk):
        columns = lax.all_to_all(
            sources[..., start : start + chunk], "col", split_axis=2, concat_axis=1, tiled=True
        ).reshape(groups, held, chunk)
        partial = lax.dot_general(
            rows,
            standardize(columns, counts, total_samples),
            (((0, 1), (0, 1)), ((), ())),
            preferred_element_type=jnp.float32,
        )
        updates.append(lax.psum_scatter(factor * partial, "row", scatter_dimension=0, tiled=True))
    return slab_in + jnp.concatenate(updates, axis=1)


def local(dosages, allele_counts, slab_in):
    groups, own, total_samples = dosages.shape
    snp_count = allele_counts.shape[1]
    rows_n = lax.axis_size("row")
    cols_n = lax.axis_size("col")
    factor = 1.0 / math.sqrt(groups * snp_count)
    held = own * cols_n
    depth = groups * own
    block_rows, width = slab_in.shape
    slab_rows = block_rows * rows_n
    wide = LANES
    chunks = width // wide
    scratch = scratch_of(depth, cols_n, max(chunks, 1), wide, slab_rows, block_rows)
    size = sum(math.prod(shape) * jnp.dtype(kind).itemsize for shape, kind in scratch)
    fits = (
        rows_n == 4
        and cols_n % 2 == 0
        and depth % LANES == 0
        and own % 16 == 0
        and held % LANES == 0
        and width % wide == 0
        and block_rows % (2 * LANES) == 0
        and chunks >= 4
        and size + 16 * 1024 * 1024 <= VMEM_BYTES
    )
    if not fits:
        counts = lax.dynamic_slice_in_dim(
            allele_counts, lax.axis_index("row") * held, held, axis=1
        )
        return chunked(
            groups, own, counts, total_samples, dosages, slab_in, factor, rows_n, cols_n
        )
    dma = pltpu.SemaphoreType.DMA
    return pl.pallas_call(
        functools.partial(kernel, factor, cols_n, chunks, own),
        out_shape=jax.ShapeDtypeStruct((block_rows, width), jnp.float32),
        in_specs=[
            pl.BlockSpec(memory_space=pl.ANY),
            pl.BlockSpec(memory_space=pl.ANY),
            pl.BlockSpec(memory_space=pl.ANY),
        ],
        out_specs=pl.BlockSpec(memory_space=pl.ANY),
        scratch_shapes=[pltpu.VMEM(allele_counts.shape, jnp.int32)]
        + [pltpu.VMEM(shape, kind) for shape, kind in scratch]
        + [
            dma((3, 4, cols_n)), dma((4, cols_n)), dma((4,)), dma((chunks,)), dma((chunks,)), dma((chunks,)),
            dma((4, chunks)), dma((4, chunks)), dma((2, chunks)), dma((2, chunks)), dma((chunks,)),
            dma((chunks,)), dma, pltpu.SemaphoreType.REGULAR((2, cols_n // 2)),
        ],
        compiler_params=pltpu.CompilerParams(
            collective_id=0, has_side_effects=True, vmem_limit_bytes=VMEM_BYTES
        ),
    )(dosages.reshape(depth, total_samples), allele_counts, slab_in)


def solution(mesh):
    placed = (P(None, ("row", "col"), None), P(), P("row", "col"))
    return jax.shard_map(
        local, mesh=mesh, in_specs=placed, out_specs=P("row", "col"), check_vma=False
    )
```

```python
import functools
import math

import jax
import jax.numpy as jnp
from jax import lax
from jax.experimental import pallas as pl
from jax.experimental.pallas import tpu as pltpu
from jax.sharding import PartitionSpec as P

LANES = 128
FILL = (0, 1, 2, 3)
LEAD = 3
LAG = 1
HEAD = 2
LATE_STEP = 2
VMEM_BYTES = 48 * 1024 * 1024
MESH = pl.DeviceIdType.MESH


def moments(count, total_samples):
    frequency = count.astype(jnp.float32) / (2.0 * total_samples)
    return 2.0 * frequency, jnp.sqrt(2.0 * frequency * (1.0 - frequency))


def standardize(dosage_block, count_row, total_samples):
    centre, spread = moments(count_row, total_samples)
    return ((dosage_block.astype(jnp.float32) - centre[..., None]) / spread[..., None]).astype(
        jnp.bfloat16
    )


def kernel(
    factor, cols_n, chunks, own,
    source, counts, slab, out,
    tally, centre, scale, rows_raw, rows_t, cols, keep_a, keep_b, final,
    send_a, send_b, got_a, got_b, send2_a, send2_b, got2_a, got2_b,
    rows_send, rows_recv, rows_own_sem, cols_send, cols_recv, cols_own,
    s1_send, s1_recv, s2_send, s2_recv, out_sem, slab_sem, tally_sem, word,
):
    r = lax.axis_index("row")
    c = lax.axis_index("col")
    depth = source.shape[0]
    chips = cols_n // 2
    core = lax.rem(c, 2)
    z = c // 2
    partner = c + 1 - 2 * core
    width = out.shape[1]
    wide = width // chunks
    block_rows = out.shape[0]
    r1 = r + 1 - 2 * lax.rem(r, 2)
    r2 = lax.rem(r + 2, 4)
    r3 = lax.rem(r1 + 2, 4)
    blocks = (r3, r1, r2, r)
    early = (0, 1, 2)
    late = 3

    def at_col(col):
        return {"row": r, "col": col}

    def at_row(row):
        return {"row": row, "col": c}

    tally_copy = pltpu.make_async_copy(counts, tally, tally_sem)
    tally_copy.start()
    barrier = pltpu.get_barrier_semaphore()
    up, down = lax.rem(c + 2, cols_n), lax.rem(c + cols_n - 2, cols_n)
    has_up, has_down = z + 1 < chips, z > 0

    def greet(semaphore, target):
        pl.semaphore_signal(semaphore, 1, device_id=target, device_id_type=MESH)

    pl.when(has_up)(lambda: greet(barrier, at_col(up)))
    pl.when(has_down)(lambda: greet(barrier, at_col(down)))
    for target in (at_col(partner), at_row(r1), at_row(r2)):
        greet(barrier, target)
    pl.semaphore_wait(barrier, 3 + has_up.astype(jnp.int32) + has_down.astype(jnp.int32))

    def ready():
        for wave in range(chips - 1):
            pl.when(has_up)(lambda: greet(word.at[0, wave], at_col(up)))
            pl.when(has_down)(lambda: greet(word.at[1, wave], at_col(down)))
            pl.when(has_down)(lambda: pl.semaphore_wait(word.at[0, wave], 1))
            pl.when(has_up)(lambda: pl.semaphore_wait(word.at[1, wave], 1))

    def slot_rows(slot):
        return pl.ds(pl.multiple_of(slot * depth, depth), depth)

    def own_block(j):
        return source.at[:, pl.ds(pl.multiple_of(blocks[j] * block_rows, block_rows), block_rows)]

    def rows_copy(j, slot, target, way, first):
        place = rows_raw.at[j, slot_rows(slot)]
        return pltpu.make_async_remote_copy(
            src_ref=own_block(j) if first else place,
            dst_ref=place,
            send_sem=rows_send.at[way, j, slot],
            recv_sem=rows_recv.at[j, slot],
            device_id=at_col(target),
            device_id_type=MESH,
        )

    def rows_arrived(j, slot):
        rows_copy(j, slot, partner, 2, False).wait_recv()

    def send_rows(j, slot, first, go_up, go_down):
        @pl.when(go_up)
        def _():
            rows_copy(j, slot, up, 0, first).start()

        @pl.when(go_down)
        def _():
            rows_copy(j, slot, down, 1, first).start()

        rows_copy(j, slot, partner, 2, first).start()

    def own_rows(j):
        return pltpu.make_async_copy(
            own_block(j), rows_raw.at[j, slot_rows(c)], rows_own_sem.at[j]
        )

    def first_rows(j):
        own_rows(j).start()
        send_rows(j, c, True, z + 1 < chips, z > 0)

    def forward_rows(j, distance):
        @pl.when(z >= distance)
        def _():
            rows_arrived(j, c - 2 * distance)
            send_rows(j, c - 2 * distance, False, z + 1 < chips, z < 0)

        @pl.when(z + distance < chips)
        def _():
            rows_arrived(j, c + 2 * distance)
            send_rows(j, c + 2 * distance, False, z < 0, z > 0)

    def columns_copy(q, step):
        target = lax.rem(c + step, cols_n)
        return pltpu.make_async_remote_copy(
            src_ref=source.at[:, pl.ds(pl.multiple_of(target * width + q * wide, wide), wide)],
            dst_ref=cols.at[q, slot_rows(c)],
            send_sem=cols_send.at[q],
            recv_sem=cols_recv.at[q],
            device_id=at_col(target),
            device_id_type=MESH,
        )

    def own_columns(q):
        return pltpu.make_async_copy(
            source.at[:, pl.ds(pl.multiple_of(c * width + q * wide, wide), wide)],
            cols.at[q, slot_rows(c)],
            cols_own.at[q],
        )

    def send_columns(q):
        for step in range(1, cols_n):
            columns_copy(q, step).start()
        own_columns(q).start()

    def turn_rows(j, slot):
        place = slot_rows(slot)
        for start in range(0, block_rows, LANES):
            raw = rows_raw[j, place, pl.ds(start, LANES)].astype(jnp.float32)
            value = (raw - centre[place, :]) * scale[place, :]
            rows_t[j, pl.ds(start, LANES), place] = value.T.astype(jnp.bfloat16)

    def turn_own(j):
        own_rows(j).wait()
        turn_rows(j, c)

    def turn_partner(j):
        rows_arrived(j, partner)
        turn_rows(j, partner)

    def turn_at(j, distance):
        @pl.when(z >= distance)
        def _():
            turn_rows(j, c - 2 * distance)
            rows_arrived(j, partner - 2 * distance)
            turn_rows(j, partner - 2 * distance)

        @pl.when(z + distance < chips)
        def _():
            turn_rows(j, c + 2 * distance)
            rows_arrived(j, partner + 2 * distance)
            turn_rows(j, partner + 2 * distance)

    for j in early:
        first_rows(j)
    tally_copy.wait()
    line = own * cols_n
    for group in range(depth // own):
        count = tally[pl.ds(group, 1), pl.ds(pl.multiple_of(r * line, LANES), line)]
        middle, spread = moments(count, source.shape[1])
        middle = jnp.broadcast_to(middle, (LANES, line)).T
        spread = jnp.broadcast_to(1.0 / spread, (LANES, line)).T
        for slot in range(cols_n):
            place = pl.ds(slot * depth + group * own, own)
            centre[place, :] = middle[slot * own : (slot + 1) * own]
            scale[place, :] = spread[slot * own : (slot + 1) * own]
    ready()
    for q in range(FILL[0]):
        send_columns(q)
    for j in early:
        turn_own(j)
    for distance in range(1, chips):
        for j in early:
            forward_rows(j, distance)
        for q in range(FILL[distance - 1], FILL[distance]):
            send_columns(q)
        for j in early:
            if distance == 1:
                turn_partner(j)
            elif distance < chips - 1:
                turn_at(j, distance - 1)

    begun = FILL[chips - 1]

    def slab_copy(q):
        place = pl.ds(pl.multiple_of(q * wide, wide), wide)
        return pltpu.make_async_copy(slab.at[:, place], final.at[q], slab_sem.at[q])

    for q in range(chunks):
        slab_copy(q).start()

    def exchange(src, dst, at, sends, recvs, q, side, row):
        return pltpu.make_async_remote_copy(
            src_ref=src.at[at],
            dst_ref=dst.at[at],
            send_sem=sends.at[side, q],
            recv_sem=recvs.at[side, q],
            device_id=at_row(row),
            device_id_type=MESH,
        )

    def far_a(q):
        return exchange(send_a, got_a, (q, 1), s1_send, s1_recv, q, 0, r1)

    def far_b(q):
        return exchange(send_b, got_b, (q, 1), s1_send, s1_recv, q, 1, r2)

    def near_a(q):
        return exchange(send_a, got_a, (q, 0), s1_send, s1_recv, q, 2, r1)

    def near_b(q):
        return exchange(send_b, got_b, (q, 0), s1_send, s1_recv, q, 3, r2)

    def second_a(q):
        return exchange(send2_a, got2_a, (q,), s2_send, s2_recv, q, 0, r2)

    def second_b(q):
        return exchange(send2_b, got2_b, (q,), s2_send, s2_recv, q, 1, r1)

    half = out.shape[0] // 2

    def columns_received(q):
        place = cols.at[q, pl.ds(0, (cols_n - 1) * depth)]
        pltpu.make_async_copy(place, place, cols_recv.at[q]).wait()
        own_columns(q).wait()

    def product(j, q):
        return jnp.dot(rows_t[j], cols[q], preferred_element_type=jnp.float32)

    def prepare(q):
        columns_received(q)
        for slot in range(cols_n):
            place = pl.ds(slot * depth, depth)
            for start in range(0, wide, LANES):
                raw = cols[q, place, pl.ds(start, LANES)].astype(jnp.float32)
                value = (raw - centre[place, :]) * scale[place, :]
                cols[q, place, pl.ds(start, LANES)] = value.astype(jnp.bfloat16)

    def make_far(q):
        far = product(0, q)
        send_a[q, 1] = far[:half].astype(jnp.bfloat16)
        far_a(q).start()
        send_b[q, 1] = far[half:].astype(jnp.bfloat16)
        far_b(q).start()

    def make_near_a(q):
        near = product(1, q)
        send_a[q, 0] = near[:half].astype(jnp.bfloat16)
        near_a(q).start()
        keep_b[lax.rem(q, LAG + HEAD)] = near[half:]

    def make_near_b(q):
        near = product(2, q)
        send_b[q, 0] = near[half:].astype(jnp.bfloat16)
        near_b(q).start()
        keep_a[lax.rem(q, LAG + HEAD)] = near[:half]

    def produce(q):
        prepare(q)
        make_far(q)
        make_near_a(q)
        make_near_b(q)

    def combine(q):
        far_a(q).wait_recv()
        send2_a[q] = (keep_a[lax.rem(q, LAG + HEAD)] + got_a[q, 1].astype(jnp.float32)).astype(jnp.bfloat16)
        second_a(q).start()
        far_b(q).wait_recv()
        send2_b[q] = (keep_b[lax.rem(q, LAG + HEAD)] + got_b[q, 1].astype(jnp.float32)).astype(jnp.bfloat16)
        second_b(q).start()

    def out_copy(q):
        place = pl.ds(pl.multiple_of(q * wide, wide), wide)
        return pltpu.make_async_copy(final.at[q], out.at[:, place], out_sem.at[q])

    def finish(q):
        own = product(late, q)
        slab_copy(q).wait()
        near_a(q).wait_recv()
        second_a(q).wait_recv()
        final[q, :half] += factor * (
            own[:half]
            + got_a[q, 0].astype(jnp.float32)
            + got2_a[q].astype(jnp.float32)
        )
        near_b(q).wait_recv()
        second_b(q).wait_recv()
        final[q, half:] += factor * (
            own[half:]
            + got_b[q, 0].astype(jnp.float32)
            + got2_b[q].astype(jnp.float32)
        )
        out_copy(q).start()

    hops = tuple(min(LATE_STEP * distance, chunks // 2) for distance in range(chips + 1))
    settle = hops[chips]

    def finished(q):
        return jnp.maximum(jnp.minimum(2 * (q - settle + 1), q - 2 * LAG + 1), 0)

    def step(q, carry):
        @pl.when((q + LEAD >= begun) & (q + LEAD < chunks))
        def _():
            send_columns(q + LEAD)

        for distance in range(1, chips):

            @pl.when(q == hops[distance])
            def _():
                forward_rows(late, distance)

        @pl.when(q < chunks)
        def _():
            produce(q)

        @pl.when(q == HEAD)
        def _():
            for back in range(HEAD, LAG, -1):
                combine(q - back)

        @pl.when(q < chunks + LAG)
        def _():
            combine(q - LAG)

        @pl.when(q == settle)
        def _():
            turn_own(late)
            turn_partner(late)
            for distance in range(1, chips):
                turn_at(late, distance)

        begin, end = finished(q - 1), finished(q)
        for extra in range(2):

            @pl.when(begin + extra < end)
            def _():
                finish(begin + extra)

        return carry

    first_rows(late)
    for q in range(HEAD):
        if begun <= q + LEAD < chunks:
            send_columns(q + LEAD)
    for j, make in zip(early, (make_far, make_near_a, make_near_b)):
        for distance in range(chips - 2, chips):
            turn_at(j, distance)
        for q in range(HEAD):
            if j == 0:
                prepare(q)
            make(q)
    lax.fori_loop(HEAD, chunks + 2 * LAG, step, 0)

    for j in range(4):
        rows_copy(j, c, partner, 2, True).wait_send()

        @pl.when(z + 1 < chips)
        def _():
            rows_copy(j, c, up, 0, True).wait_send()

        @pl.when(z > 0)
        def _():
            rows_copy(j, c, down, 1, True).wait_send()

        for distance in range(1, chips):
            below, above = c - 2 * distance, c + 2 * distance

            @pl.when(z >= distance)
            def _():
                rows_copy(j, below, partner, 2, False).wait_send()

            @pl.when((z >= distance) & (z + 1 < chips))
            def _():
                rows_copy(j, below, up, 0, False).wait_send()

            @pl.when(z + distance < chips)
            def _():
                rows_copy(j, above, partner, 2, False).wait_send()

            @pl.when((z + distance < chips) & (z > 0))
            def _():
                rows_copy(j, above, down, 1, False).wait_send()

    def drain(q, carry):
        sent = cols.at[q, pl.ds(0, (cols_n - 1) * depth)]
        pltpu.make_async_copy(sent, sent, cols_send.at[q]).wait()
        far_a(q).wait_send()
        far_b(q).wait_send()
        near_a(q).wait_send()
        near_b(q).wait_send()
        second_a(q).wait_send()
        second_b(q).wait_send()
        out_copy(q).wait()
        return carry

    lax.fori_loop(0, chunks, drain, 0)


def scratch_of(depth, cols_n, chunks, wide, slab_rows, block_rows):
    held = depth * cols_n
    half = block_rows // 2
    bf16, f32 = jnp.bfloat16, jnp.float32
    return [
        ((held, LANES), f32),
        ((held, LANES), f32),
        ((slab_rows // block_rows, held, block_rows), bf16),
        ((slab_rows // block_rows, block_rows, held), bf16),
        ((chunks, held, wide), bf16),
        ((LAG + HEAD, half, wide), f32),
        ((LAG + HEAD, half, wide), f32),
        ((chunks, block_rows, wide), f32),
        ((chunks, 2, half, wide), bf16),
        ((chunks, 2, half, wide), bf16),
        ((chunks, 2, half, wide), bf16),
        ((chunks, 2, half, wide), bf16),
        ((chunks, half, wide), bf16),
        ((chunks, half, wide), bf16),
        ((chunks, half, wide), bf16),
        ((chunks, half, wide), bf16),
    ]


def chunked(groups, own, counts, total_samples, dosages, slab_in, factor, rows_n, cols_n):
    held = own * cols_n
    slab_rows = slab_in.shape[0] * rows_n
    rows = lax.all_gather(dosages[:, :, :slab_rows], "col", axis=1, tiled=True)
    rows = standardize(rows, counts, total_samples)
    width = slab_in.shape[1]
    chunk = min(1024, width)
    sources = dosages.reshape(groups, own, cols_n, width)
    updates = []
    for start in range(0, width, chunk):
        columns = lax.all_to_all(
            sources[..., start : start + chunk], "col", split_axis=2, concat_axis=1, tiled=True
        ).reshape(groups, held, chunk)
        partial = lax.dot_general(
            rows,
            standardize(columns, counts, total_samples),
            (((0, 1), (0, 1)), ((), ())),
            preferred_element_type=jnp.float32,
        )
        updates.append(lax.psum_scatter(factor * partial, "row", scatter_dimension=0, tiled=True))
    return slab_in + jnp.concatenate(updates, axis=1)


def local(dosages, allele_counts, slab_in):
    groups, own, total_samples = dosages.shape
    snp_count = allele_counts.shape[1]
    rows_n = lax.axis_size("row")
    cols_n = lax.axis_size("col")
    factor = 1.0 / math.sqrt(groups * snp_count)
    held = own * cols_n
    depth = groups * own
    block_rows, width = slab_in.shape
    slab_rows = block_rows * rows_n
    wide = LANES
    chunks = width // wide
    scratch = scratch_of(depth, cols_n, max(chunks, 1), wide, slab_rows, block_rows)
    size = sum(math.prod(shape) * jnp.dtype(kind).itemsize for shape, kind in scratch)
    fits = (
        rows_n == 4
        and cols_n % 2 == 0
        and depth % LANES == 0
        and own % 16 == 0
        and held % LANES == 0
        and width % wide == 0
        and block_rows % (2 * LANES) == 0
        and chunks >= 4
        and size + 16 * 1024 * 1024 <= VMEM_BYTES
    )
    if not fits:
        counts = lax.dynamic_slice_in_dim(
            allele_counts, lax.axis_index("row") * held, held, axis=1
        )
        return chunked(
            groups, own, counts, total_samples, dosages, slab_in, factor, rows_n, cols_n
        )
    dma = pltpu.SemaphoreType.DMA
    return pl.pallas_call(
        functools.partial(kernel, factor, cols_n, chunks, own),
        out_shape=jax.ShapeDtypeStruct((block_rows, width), jnp.float32),
        in_specs=[
            pl.BlockSpec(memory_space=pl.ANY),
            pl.BlockSpec(memory_space=pl.ANY),
            pl.BlockSpec(memory_space=pl.ANY),
        ],
        out_specs=pl.BlockSpec(memory_space=pl.ANY),
        scratch_shapes=[pltpu.VMEM(allele_counts.shape, jnp.int32)]
        + [pltpu.VMEM(shape, kind) for shape, kind in scratch]
        + [
            dma((3, 4, cols_n)), dma((4, cols_n)), dma((4,)), dma((chunks,)), dma((chunks,)), dma((chunks,)),
            dma((4, chunks)), dma((4, chunks)), dma((2, chunks)), dma((2, chunks)), dma((chunks,)),
            dma((chunks,)), dma, pltpu.SemaphoreType.REGULAR((2, cols_n // 2)),
        ],
        compiler_params=pltpu.CompilerParams(
            collective_id=0, has_side_effects=True, vmem_limit_bytes=VMEM_BYTES
        ),
    )(dosages.reshape(depth, total_samples), allele_counts, slab_in)


def solution(mesh):
    placed = (P(None, ("row", "col"), None), P(), P("row", "col"))
    return jax.shard_map(
        local, mesh=mesh, in_specs=placed, out_specs=P("row", "col"), check_vma=False
    )
```

```python
import functools
import math

import jax
import jax.numpy as jnp
from jax import lax
from jax.experimental import pallas as pl
from jax.experimental.pallas import tpu as pltpu
from jax.sharding import PartitionSpec as P

LANES = 128
FILL = (0, 1, 2, 3)
LEAD = 3
LAG = 1
HEAD = 2
VMEM_BYTES = 48 * 1024 * 1024
MESH = pl.DeviceIdType.MESH


def moments(count, total_samples):
    frequency = count.astype(jnp.float32) / (2.0 * total_samples)
    return 2.0 * frequency, jnp.sqrt(2.0 * frequency * (1.0 - frequency))


def standardize(dosage_block, count_row, total_samples):
    centre, spread = moments(count_row, total_samples)
    return ((dosage_block.astype(jnp.float32) - centre[..., None]) / spread[..., None]).astype(
        jnp.bfloat16
    )


def kernel(
    factor, cols_n, chunks, own,
    source, counts, slab, out,
    tally, centre, scale, rows_raw, rows_t, cols, keep_a, keep_b, final,
    send_a, send_b, got_a, got_b, send2_a, send2_b, got2_a, got2_b,
    rows_send, rows_recv, rows_own_sem, cols_send, cols_recv, cols_own,
    s1_send, s1_recv, s2_send, s2_recv, out_sem, slab_sem, tally_sem, word,
):
    r = lax.axis_index("row")
    c = lax.axis_index("col")
    depth = source.shape[0]
    chips = cols_n // 2
    core = lax.rem(c, 2)
    z = c // 2
    partner = c + 1 - 2 * core
    width = out.shape[1]
    wide = width // chunks
    block_rows = out.shape[0]
    r1 = r + 1 - 2 * lax.rem(r, 2)
    r2 = lax.rem(r + 2, 4)
    r3 = lax.rem(r1 + 2, 4)
    blocks = (r3, r1, r2, r)
    early = (0, 1, 2)
    late = 3

    def at_col(col):
        return {"row": r, "col": col}

    def at_row(row):
        return {"row": row, "col": c}

    tally_copy = pltpu.make_async_copy(counts, tally, tally_sem)
    tally_copy.start()
    barrier = pltpu.get_barrier_semaphore()
    up, down = lax.rem(c + 2, cols_n), lax.rem(c + cols_n - 2, cols_n)
    has_up, has_down = z + 1 < chips, z > 0

    def greet(semaphore, target):
        pl.semaphore_signal(semaphore, 1, device_id=target, device_id_type=MESH)

    pl.when(has_up)(lambda: greet(barrier, at_col(up)))
    pl.when(has_down)(lambda: greet(barrier, at_col(down)))
    for target in (at_col(partner), at_row(r1), at_row(r2)):
        greet(barrier, target)
    pl.semaphore_wait(barrier, 3 + has_up.astype(jnp.int32) + has_down.astype(jnp.int32))

    def tell(wave):
        pl.when(has_up)(lambda: greet(word.at[0, wave], at_col(up)))
        pl.when(has_down)(lambda: greet(word.at[1, wave], at_col(down)))

    def hear(wave):
        pl.when(has_down)(lambda: pl.semaphore_wait(word.at[0, wave], 1))
        pl.when(has_up)(lambda: pl.semaphore_wait(word.at[1, wave], 1))

    def slot_rows(slot):
        return pl.ds(pl.multiple_of(slot * depth, depth), depth)

    def own_block(j):
        return source.at[:, pl.ds(pl.multiple_of(blocks[j] * block_rows, block_rows), block_rows)]

    def rows_copy(j, slot, target, way, first):
        place = rows_raw.at[j, slot_rows(slot)]
        return pltpu.make_async_remote_copy(
            src_ref=own_block(j) if first else place,
            dst_ref=place,
            send_sem=rows_send.at[way, j, slot],
            recv_sem=rows_recv.at[j, slot],
            device_id=at_col(target),
            device_id_type=MESH,
        )

    def rows_arrived(j, slot):
        rows_copy(j, slot, partner, 2, False).wait_recv()

    def send_rows(j, slot, first, go_up, go_down):
        @pl.when(go_up)
        def _():
            rows_copy(j, slot, up, 0, first).start()

        @pl.when(go_down)
        def _():
            rows_copy(j, slot, down, 1, first).start()

        rows_copy(j, slot, partner, 2, first).start()

    def own_rows(j):
        return pltpu.make_async_copy(
            own_block(j), rows_raw.at[j, slot_rows(c)], rows_own_sem.at[j]
        )

    def first_rows(j):
        own_rows(j).start()
        send_rows(j, c, True, z + 1 < chips, z > 0)

    def forward_rows(j, distance):
        @pl.when(z >= distance)
        def _():
            rows_arrived(j, c - 2 * distance)
            send_rows(j, c - 2 * distance, False, z + 1 < chips, z < 0)

        @pl.when(z + distance < chips)
        def _():
            rows_arrived(j, c + 2 * distance)
            send_rows(j, c + 2 * distance, False, z < 0, z > 0)

    def columns_copy(q, step):
        target = lax.rem(c + step, cols_n)
        return pltpu.make_async_remote_copy(
            src_ref=source.at[:, pl.ds(pl.multiple_of(target * width + q * wide, wide), wide)],
            dst_ref=cols.at[q, slot_rows(c)],
            send_sem=cols_send.at[q],
            recv_sem=cols_recv.at[q],
            device_id=at_col(target),
            device_id_type=MESH,
        )

    def own_columns(q):
        return pltpu.make_async_copy(
            source.at[:, pl.ds(pl.multiple_of(c * width + q * wide, wide), wide)],
            cols.at[q, slot_rows(c)],
            cols_own.at[q],
        )

    def send_columns(q):
        for step in range(1, cols_n):
            columns_copy(q, step).start()
        own_columns(q).start()

    def turn_rows(j, slot):
        place = slot_rows(slot)
        for start in range(0, block_rows, LANES):
            raw = rows_raw[j, place, pl.ds(start, LANES)].astype(jnp.float32)
            value = (raw - centre[place, :]) * scale[place, :]
            rows_t[j, pl.ds(start, LANES), place] = value.T.astype(jnp.bfloat16)

    def turn_own(j):
        own_rows(j).wait()
        turn_rows(j, c)

    def turn_partner(j):
        rows_arrived(j, partner)
        turn_rows(j, partner)

    def turn_at(j, distance):
        @pl.when(z >= distance)
        def _():
            turn_rows(j, c - 2 * distance)
            rows_arrived(j, partner - 2 * distance)
            turn_rows(j, partner - 2 * distance)

        @pl.when(z + distance < chips)
        def _():
            turn_rows(j, c + 2 * distance)
            rows_arrived(j, partner + 2 * distance)
            turn_rows(j, partner + 2 * distance)

    for j in early:
        first_rows(j)
    tell(0)
    tally_copy.wait()
    line = own * cols_n
    for group in range(depth // own):
        count = tally[pl.ds(group, 1), pl.ds(pl.multiple_of(r * line, LANES), line)]
        middle, spread = moments(count, source.shape[1])
        middle = jnp.broadcast_to(middle, (LANES, line)).T
        spread = jnp.broadcast_to(1.0 / spread, (LANES, line)).T
        for slot in range(cols_n):
            place = pl.ds(slot * depth + group * own, own)
            centre[place, :] = middle[slot * own : (slot + 1) * own]
            scale[place, :] = spread[slot * own : (slot + 1) * own]
    for wave in range(1, chips - 1):
        hear(wave - 1)
        tell(wave)
        if wave == 1:
            for j in early:
                turn_own(j)
    for distance in range(1, chips):
        for j in early:
            forward_rows(j, distance)
        if distance == 1:
            hear(chips - 2)
        for q in range(FILL[distance - 1], FILL[distance]):
            send_columns(q)
        for j in early:
            if distance == 1:
                turn_partner(j)
            elif distance < chips - 1:
                turn_at(j, distance - 1)

    begun = FILL[chips - 1]

    def slab_copy(q):
        place = pl.ds(pl.multiple_of(q * wide, wide), wide)
        return pltpu.make_async_copy(slab.at[:, place], final.at[q], slab_sem.at[q])

    for q in range(chunks):
        slab_copy(q).start()

    def exchange(src, dst, at, sends, recvs, q, side, row):
        return pltpu.make_async_remote_copy(
            src_ref=src.at[at],
            dst_ref=dst.at[at],
            send_sem=sends.at[side, q],
            recv_sem=recvs.at[side, q],
            device_id=at_row(row),
            device_id_type=MESH,
        )

    def far_a(q):
        return exchange(send_a, got_a, (q, 1), s1_send, s1_recv, q, 0, r1)

    def far_b(q):
        return exchange(send_b, got_b, (q, 1), s1_send, s1_recv, q, 1, r2)

    def near_a(q):
        return exchange(send_a, got_a, (q, 0), s1_send, s1_recv, q, 2, r1)

    def near_b(q):
        return exchange(send_b, got_b, (q, 0), s1_send, s1_recv, q, 3, r2)

    def second_a(q):
        return exchange(send2_a, got2_a, (q,), s2_send, s2_recv, q, 0, r2)

    def second_b(q):
        return exchange(send2_b, got2_b, (q,), s2_send, s2_recv, q, 1, r1)

    half = out.shape[0] // 2

    def columns_received(q):
        place = cols.at[q, pl.ds(0, (cols_n - 1) * depth)]
        pltpu.make_async_copy(place, place, cols_recv.at[q]).wait()
        own_columns(q).wait()

    def product(j, q):
        return jnp.dot(rows_t[j], cols[q], preferred_element_type=jnp.float32)

    def prepare(q):
        columns_received(q)
        for slot in range(cols_n):
            place = pl.ds(slot * depth, depth)
            for start in range(0, wide, LANES):
                raw = cols[q, place, pl.ds(start, LANES)].astype(jnp.float32)
                value = (raw - centre[place, :]) * scale[place, :]
                cols[q, place, pl.ds(start, LANES)] = value.astype(jnp.bfloat16)

    def make_far(q):
        far = product(0, q)
        send_a[q, 1] = far[:half].astype(jnp.bfloat16)
        far_a(q).start()
        send_b[q, 1] = far[half:].astype(jnp.bfloat16)
        far_b(q).start()

    def make_near_a(q):
        near = product(1, q)
        send_a[q, 0] = near[:half].astype(jnp.bfloat16)
        near_a(q).start()
        keep_b[lax.rem(q, LAG + HEAD)] = near[half:]

    def make_near_b(q):
        near = product(2, q)
        send_b[q, 0] = near[half:].astype(jnp.bfloat16)
        near_b(q).start()
        keep_a[lax.rem(q, LAG + HEAD)] = near[:half]

    def produce(q):
        prepare(q)
        make_far(q)
        make_near_a(q)
        make_near_b(q)

    def combine(q):
        far_a(q).wait_recv()
        send2_a[q] = (keep_a[lax.rem(q, LAG + HEAD)] + got_a[q, 1].astype(jnp.float32)).astype(jnp.bfloat16)
        second_a(q).start()
        far_b(q).wait_recv()
        send2_b[q] = (keep_b[lax.rem(q, LAG + HEAD)] + got_b[q, 1].astype(jnp.float32)).astype(jnp.bfloat16)
        second_b(q).start()

    def out_copy(q):
        place = pl.ds(pl.multiple_of(q * wide, wide), wide)
        return pltpu.make_async_copy(final.at[q], out.at[:, place], out_sem.at[q])

    def finish(q):
        own = product(late, q)
        slab_copy(q).wait()
        near_a(q).wait_recv()
        second_a(q).wait_recv()
        final[q, :half] += factor * (
            own[:half]
            + got_a[q, 0].astype(jnp.float32)
            + got2_a[q].astype(jnp.float32)
        )
        near_b(q).wait_recv()
        second_b(q).wait_recv()
        final[q, half:] += factor * (
            own[half:]
            + got_b[q, 0].astype(jnp.float32)
            + got2_b[q].astype(jnp.float32)
        )
        out_copy(q).start()

    hops = [min(HEAD + distance - 1, chunks // 2) for distance in range(chips)]
    settle = min(HEAD + chips, chunks // 2)

    def finished(q):
        return jnp.maximum(jnp.minimum(2 * (q - settle + 1), q - 2 * LAG + 1), 0)

    def step(q, carry):
        @pl.when((q + LEAD >= begun) & (q + LEAD < chunks))
        def _():
            send_columns(q + LEAD)

        for distance in range(1, chips):

            @pl.when(q == hops[distance])
            def _():
                forward_rows(late, distance)

        @pl.when(q < chunks)
        def _():
            produce(q)

        @pl.when(q == HEAD)
        def _():
            for back in range(HEAD, LAG, -1):
                combine(q - back)

        @pl.when(q < chunks + LAG)
        def _():
            combine(q - LAG)

        @pl.when(q == settle)
        def _():
            turn_own(late)
            turn_partner(late)
            for distance in range(1, chips):
                turn_at(late, distance)

        begin, end = finished(q - 1), finished(q)
        for extra in range(2):

            @pl.when(begin + extra < end)
            def _():
                finish(begin + extra)

        return carry

    first_rows(late)
    for q in range(HEAD):
        if begun <= q + LEAD < chunks:
            send_columns(q + LEAD)
    for j, make in zip(early, (make_far, make_near_a, make_near_b)):
        for distance in range(chips - 2, chips):
            turn_at(j, distance)
        for q in range(HEAD):
            if j == 0:
                prepare(q)
            make(q)
    lax.fori_loop(HEAD, chunks + 2 * LAG, step, 0)

    for j in range(4):
        rows_copy(j, c, partner, 2, True).wait_send()

        @pl.when(z + 1 < chips)
        def _():
            rows_copy(j, c, up, 0, True).wait_send()

        @pl.when(z > 0)
        def _():
            rows_copy(j, c, down, 1, True).wait_send()

        for distance in range(1, chips):
            below, above = c - 2 * distance, c + 2 * distance

            @pl.when(z >= distance)
            def _():
                rows_copy(j, below, partner, 2, False).wait_send()

            @pl.when((z >= distance) & (z + 1 < chips))
            def _():
                rows_copy(j, below, up, 0, False).wait_send()

            @pl.when(z + distance < chips)
            def _():
                rows_copy(j, above, partner, 2, False).wait_send()

            @pl.when((z + distance < chips) & (z > 0))
            def _():
                rows_copy(j, above, down, 1, False).wait_send()

    def drain(q, carry):
        sent = cols.at[q, pl.ds(0, (cols_n - 1) * depth)]
        pltpu.make_async_copy(sent, sent, cols_send.at[q]).wait()
        far_a(q).wait_send()
        far_b(q).wait_send()
        near_a(q).wait_send()
        near_b(q).wait_send()
        second_a(q).wait_send()
        second_b(q).wait_send()
        out_copy(q).wait()
        return carry

    lax.fori_loop(0, chunks, drain, 0)


def scratch_of(depth, cols_n, chunks, wide, slab_rows, block_rows):
    held = depth * cols_n
    half = block_rows // 2
    bf16, f32 = jnp.bfloat16, jnp.float32
    return [
        ((held, LANES), f32),
        ((held, LANES), f32),
        ((slab_rows // block_rows, held, block_rows), bf16),
        ((slab_rows // block_rows, block_rows, held), bf16),
        ((chunks, held, wide), bf16),
        ((LAG + HEAD, half, wide), f32),
        ((LAG + HEAD, half, wide), f32),
        ((chunks, block_rows, wide), f32),
        ((chunks, 2, half, wide), bf16),
        ((chunks, 2, half, wide), bf16),
        ((chunks, 2, half, wide), bf16),
        ((chunks, 2, half, wide), bf16),
        ((chunks, half, wide), bf16),
        ((chunks, half, wide), bf16),
        ((chunks, half, wide), bf16),
        ((chunks, half, wide), bf16),
    ]


def chunked(groups, own, counts, total_samples, dosages, slab_in, factor, rows_n, cols_n):
    held = own * cols_n
    slab_rows = slab_in.shape[0] * rows_n
    rows = lax.all_gather(dosages[:, :, :slab_rows], "col", axis=1, tiled=True)
    rows = standardize(rows, counts, total_samples)
    width = slab_in.shape[1]
    chunk = min(1024, width)
    sources = dosages.reshape(groups, own, cols_n, width)
    updates = []
    for start in range(0, width, chunk):
        columns = lax.all_to_all(
            sources[..., start : start + chunk], "col", split_axis=2, concat_axis=1, tiled=True
        ).reshape(groups, held, chunk)
        partial = lax.dot_general(
            rows,
            standardize(columns, counts, total_samples),
            (((0, 1), (0, 1)), ((), ())),
            preferred_element_type=jnp.float32,
        )
        updates.append(lax.psum_scatter(factor * partial, "row", scatter_dimension=0, tiled=True))
    return slab_in + jnp.concatenate(updates, axis=1)


def local(dosages, allele_counts, slab_in):
    groups, own, total_samples = dosages.shape
    snp_count = allele_counts.shape[1]
    rows_n = lax.axis_size("row")
    cols_n = lax.axis_size("col")
    factor = 1.0 / math.sqrt(groups * snp_count)
    held = own * cols_n
    depth = groups * own
    block_rows, width = slab_in.shape
    slab_rows = block_rows * rows_n
    wide = LANES
    chunks = width // wide
    scratch = scratch_of(depth, cols_n, max(chunks, 1), wide, slab_rows, block_rows)
    size = sum(math.prod(shape) * jnp.dtype(kind).itemsize for shape, kind in scratch)
    fits = (
        rows_n == 4
        and cols_n == 2 * len(FILL)
        and depth % LANES == 0
        and own % 16 == 0
        and held % LANES == 0
        and width % wide == 0
        and block_rows % (2 * LANES) == 0
        and chunks >= 4
        and size + 16 * 1024 * 1024 <= VMEM_BYTES
    )
    if not fits:
        counts = lax.dynamic_slice_in_dim(
            allele_counts, lax.axis_index("row") * held, held, axis=1
        )
        return chunked(
            groups, own, counts, total_samples, dosages, slab_in, factor, rows_n, cols_n
        )
    dma = pltpu.SemaphoreType.DMA
    return pl.pallas_call(
        functools.partial(kernel, factor, cols_n, chunks, own),
        out_shape=jax.ShapeDtypeStruct((block_rows, width), jnp.float32),
        in_specs=[
            pl.BlockSpec(memory_space=pl.ANY),
            pl.BlockSpec(memory_space=pl.ANY),
            pl.BlockSpec(memory_space=pl.ANY),
        ],
        out_specs=pl.BlockSpec(memory_space=pl.ANY),
        scratch_shapes=[pltpu.VMEM(allele_counts.shape, jnp.int32)]
        + [pltpu.VMEM(shape, kind) for shape, kind in scratch]
        + [
            dma((3, 4, cols_n)), dma((4, cols_n)), dma((4,)), dma((chunks,)), dma((chunks,)), dma((chunks,)),
            dma((4, chunks)), dma((4, chunks)), dma((2, chunks)), dma((2, chunks)), dma((chunks,)),
            dma((chunks,)), dma, pltpu.SemaphoreType.REGULAR((2, cols_n // 2)),
        ],
        compiler_params=pltpu.CompilerParams(
            collective_id=0, has_side_effects=True, vmem_limit_bytes=VMEM_BYTES
        ),
    )(dosages.reshape(depth, total_samples), allele_counts, slab_in)


def solution(mesh):
    placed = (P(None, ("row", "col"), None), P(), P("row", "col"))
    return jax.shard_map(
        local, mesh=mesh, in_specs=placed, out_specs=P("row", "col"), check_vma=False
    )
```
